256 devices in a mesh: pipe: 32 (over y_hi, z, core), ctx: 8 (over x, y_lo).
Axes of the slice: x: 4, y: 4 (y_hi: 2, y_lo: 2; y = y_hi * 2 + y_lo), z: 8, core: 2. Of those that a mesh axis runs over, the one named last changes fastest.
Arguments:
- query: bfloat16 [32, 1024, 8192], P('pipe', 'ctx'), may hold values from -6 to 6
- inner: bfloat16 [32, 1024, 8192], P('pipe', 'ctx'), may hold values from -6 to 6
- out_grad: bfloat16 [32, 1024, 8192], P('pipe', 'ctx'), may hold values from -6 to 6
- filters: float32 [32, 7, 8192], P('pipe'), as said below
- trace_lengths: int32 [32, 2], P('pipe'), may hold values from 1 to 960, 1024 in all within a row
Outputs:
- passed_grad: bfloat16 [2, 32, 1024, 8192], P(None, 'pipe', 'ctx')
- filter_grad: float32 [32, 7, 8192], P('pipe', None, 'ctx')
The draws below stay inside these ranges and needn't reach their ends.
Inputs may be any that keep to these rules, and one draw needn't show every extreme that they name: filters of section s and section 31 - s are equal (the same layer).
All inputs are finite; a program needn't handle non-finite values.
Results may differ from the reference program's by a relative error of at most 0.0041.
Values may be sent and summed in bfloat16 or wider, within the bound.
No kernel may reach another device: no remote copies, remote signals or barrier semaphores. Data moves between devices by JAX's collectives and lax.ppermute only.
A program may use at most 128 MiB of HBM per device.

```python
import math
import jax
import jax.numpy as jnp
import numpy as np
from jax import lax

D = 8192
K = 7
NSEG = 2
TOK_DEV = 128
TOKENS = 1024
N_PIPE = 32


def draw_filters(key, part):
    half = jnp.clip(jax.random.normal(key, (N_PIPE // 2, K, D), jnp.float32) * 0.4, -1.6, 1.6)
    return jnp.concatenate([half, half[::-1]], axis=0)


def levels(stream_key, shape, shards, smallest, top_value):
    gain, own = 1.0, jax.random.fold_in(stream_key, 6)
    for dim, shards_of in shards:
        draws = jnp.exp(jax.random.uniform(jax.random.fold_in(own, dim), (shards_of,), jnp.float32, smallest / len(shards), top_value / len(shards)))
        gain = gain * jnp.repeat(draws, shape[dim] // shards_of).reshape([-1 if axis == dim else 1 for axis in range(len(shape))])
    return gain


def profile(count, total, bound, skew):
    weights = [(1 << 20) // math.isqrt(grade ** skew) + 1 for grade in range(2, count + 1)]
    surplus, holding = total - bound - (count - 1), [1] * (count - 1)
    while surplus > 0:
        movable = [i for i in range(count - 1) if holding[i] < bound]
        pool, remaining = sum([weights[i] for i in movable]), surplus
        for i in movable:
            extra = min(bound - holding[i], max(1, remaining * weights[i] // pool), surplus)
            holding[i] = holding[i] + extra
            surplus = surplus - extra
    return np.array([bound] + holding)


def ragged(rng, amount, total, limit, lean):
    if amount == 2:
        one = jax.random.randint(rng, (), max(1, total - limit), min(limit, total - 1) + 1)
        return jnp.stack([one, total - one])
    tallies = jnp.asarray(profile(amount, total, limit, lean), jnp.int32)
    couples = (amount - 1) // 2
    giver, sink = tallies[1:1 + 2 * couples:2], tallies[2:2 + 2 * couples:2]
    slack = jnp.minimum(giver - 1, limit - sink)
    shifted = jax.random.randint(jax.random.fold_in(rng, 1), (couples,), 0, 1 << 20) % (slack + 1)
    tallies = tallies.at[1:1 + 2 * couples:2].set(giver - shifted).at[2:2 + 2 * couples:2].set(sink + shifted)
    return tallies[jax.random.permutation(jax.random.fold_in(rng, 2), amount)]


def noise(stream_key, dims, deviation, most, cuts=(), kind=jnp.bfloat16):
    values = jax.random.normal(stream_key, dims, jnp.float32) * deviation
    if len(cuts) > 0:
        values = levels(stream_key, dims, cuts, -0.22, 0.18) * values
    return jnp.clip(values, min=-most, max=most).astype(kind)


def setup_inputs(seed: int = 0) -> dict:
    keys = jax.random.split(jax.random.key(seed), 6)
    return {
        "query": noise(keys[0], (N_PIPE, TOKENS, D), 1.0, 6.0, ((0, 32), (1, 8))),
        "inner": noise(keys[1], (N_PIPE, TOKENS, D), 1.0, 6.0, ((0, 32), (1, 8))),
        "out_grad": noise(keys[2], (N_PIPE, TOKENS, D), 1.0, 6.0, ((0, 32), (1, 8))),
        "filters": draw_filters(jax.random.fold_in(keys[5], 71), 0),
        "trace_lengths": jax.vmap(lambda own: ragged(own, NSEG, TOKENS, TOKENS - TOK_DEV // 2, 0))(jax.random.split(keys[4], N_PIPE)).reshape((N_PIPE, NSEG)).astype(jnp.int32),
    }


def seg_of(pos, ends):
    return jnp.sum((pos[:, None] >= ends[None, :]).astype(jnp.int32), axis=1)


def section_grads(items):
    query, inner, out_grad, filters, lengths = items
    ends = jnp.cumsum(lengths).astype(jnp.int32)
    pos = jnp.arange(TOKENS, dtype=jnp.int32)
    seg = seg_of(pos, ends)
    inner_f = inner.astype(jnp.float32)
    out_f = out_grad.astype(jnp.float32)
    gz = (out_f * query.astype(jnp.float32)).astype(jnp.bfloat16)
    gz_f = gz.astype(jnp.float32)
    zsum = jnp.zeros((TOKENS, D), jnp.float32)
    usum = jnp.zeros((TOKENS, D), jnp.float32)
    taps = []
    for j in range(K):
        back_u = jnp.concatenate([jnp.zeros((j, D), jnp.float32), inner_f[:TOKENS - j]], axis=0)
        back_seg = seg_of(pos - j, ends)
        mask_b = (seg == back_seg).astype(jnp.float32)[:, None]
        zsum = zsum + filters[j][None, :] * back_u * mask_b
        taps.append(jnp.sum(gz_f * back_u * mask_b, axis=0))
        ahead_g = jnp.concatenate([gz_f[j:], jnp.zeros((j, D), jnp.float32)], axis=0)
        ahead_seg = seg_of(pos + j, ends)
        mask_a = (seg == ahead_seg).astype(jnp.float32)[:, None]
        usum = usum + filters[j][None, :] * ahead_g * mask_a
    grad_q = (out_f * zsum).astype(jnp.bfloat16)
    grad_u = usum.astype(jnp.bfloat16)
    return grad_q, grad_u, jnp.stack(taps)


def reference(query, inner, out_grad, filters, trace_lengths):
    grad_q, grad_u, taps = lax.map(section_grads, (query, inner, out_grad, filters, trace_lengths))
    filter_grad = taps + taps[::-1]
    both = jnp.stack([grad_q, grad_u])
    tail = jnp.zeros((2, 1, TOKENS, D), jnp.bfloat16)
    passed_grad = jnp.concatenate([both[:, 1:], tail], axis=1)
    return passed_grad, filter_grad
```

```python
import functools

import jax
import jax.numpy as jnp
from jax import lax
from jax.experimental import pallas as pl
from jax.experimental.pallas import tpu as pltpu
from jax.sharding import PartitionSpec as P


SUB = 8
LANES = 128
EDGE = 16
HALO = 8
RANGES = ((2, 1024), (3, 1024), (3, 1024))


def f32(x):
    return x.astype(jnp.float32)


def rounded_product(a, b):
    return f32((f32(a) * f32(b)).astype(jnp.bfloat16))


def tap_rows(f_ref, lanes, taps):
    return [jnp.broadcast_to(f_ref[j, :, lanes], (SUB, LANES)) for j in range(taps)]


def back_parts(ref, row, taps, since):
    out = []
    for j in range(taps):
        part = ref[pl.ds(row - j, SUB), :]
        if since is not None and j > 0:
            part = jnp.where((since < 0) | (since >= j), part, 0.0)
        out.append(part)
    return out


def ahead_parts(ref, row, taps, since):
    out = []
    for j in range(taps):
        part = ref[pl.ds(row + j, SUB), :]
        if since is not None and j > 0:
            part = jnp.where((since >= 0) | (since < -j), part, 0.0)
        out.append(part)
    return out


def weighted(parts, f_rows):
    total = f_rows[0] * parts[0]
    for part, row in zip(parts[1:], f_rows[1:], strict=True):
        total = total + row * part
    return total


def store_pair(ref, which, row, lanes, low, high):
    ref[which, pl.ds(row, 2 * SUB), lanes] = jnp.concatenate([low, high], axis=0).astype(jnp.bfloat16)


def boundary(lengths_ref, rows, ctx):
    return lengths_ref[0, 0] - ctx * rows


def by_boundary(cut, rows, taps, body, count):
    near = (cut > -taps) & (cut < rows + taps)

    @pl.when(near)
    def _():
        lax.fori_loop(0, count, functools.partial(body, True), 0)

    @pl.when(jnp.logical_not(near))
    def _():
        lax.fori_loop(0, count, functools.partial(body, False), 0)


def main_kernel(taps, lengths_ref, f_ref, q_ref, u_ref, g_ref, *rest):
    y_ref, dh_ref, _, u_rows, gz_rows = rest[-5:]
    rows, width = q_ref.shape
    n_tiles, n_edge = rows // SUB, EDGE // SUB
    cut = boundary(lengths_ref, rows, lax.axis_index("ctx"))

    def column(masked, i, carry):
        lanes = pl.ds(pl.multiple_of(i * LANES, LANES), LANES)
        row_id = lax.broadcasted_iota(jnp.int32, (SUB, LANES), 0)
        f_rows = tap_rows(f_ref, lanes, taps)
        for k in range(0, n_tiles, 2):
            two = pl.ds(k * SUB, 2 * SUB)
            u_rows[two, :] = f32(u_ref[two, lanes])
            gz_rows[two, :] = rounded_product(g_ref[two, lanes], q_ref[two, lanes])
        acc = [jnp.zeros((SUB, LANES), jnp.float32) for _ in range(taps)]
        for k in range(0, n_tiles, 2):
            g_two = f32(g_ref[pl.ds(k * SUB, 2 * SUB), lanes])
            grads_q, grads_u = [], []
            for half in range(2):
                row = (k + half) * SUB
                since = row_id + (row - cut) if masked else None
                if k >= n_edge:
                    parts = back_parts(u_rows, row, taps, since)
                    gz_here = gz_rows[pl.ds(row, SUB), :]
                    for j in range(taps):
                        acc[j] = acc[j] + gz_here * parts[j]
                    grads_q.append(g_two[half * SUB : (half + 1) * SUB] * weighted(parts, f_rows))
                if k < n_tiles - n_edge:
                    grads_u.append(weighted(ahead_parts(gz_rows, row, taps, since), f_rows))
            if grads_q:
                store_pair(y_ref, 0, (k - n_edge) * SUB, lanes, *grads_q)
            if grads_u:
                store_pair(y_ref, 1, k * SUB, lanes, *grads_u)
        for j in range(taps):
            dh_ref[0, pl.ds(j, 1), lanes] = jnp.sum(acc[j], axis=0, keepdims=True)
        return carry

    by_boundary(cut, rows, taps, column, width // LANES)


def edge_kernel(taps, rows, lengths_ref, f_ref, q_hbm, u_hbm, g_hbm, left, right, dh_in, y_hbm, dh_out, *scratch):
    q_lo, u_lo, g_lo, q_hi, g_hi, dh_sums, y_ref, u_rows, gz_rows, sems = scratch
    n_edge = EDGE // SUB
    per_shard = dh_in.shape[2] // LANES
    cut = boundary(lengths_ref, rows, lax.axis_index("ctx"))
    low, high = pl.ds(0, EDGE), pl.ds(rows - EDGE, EDGE)
    pairs = [
        (q_hbm.at[low], q_lo), (u_hbm.at[low], u_lo), (g_hbm.at[low], g_lo), (q_hbm.at[high], q_hi), (g_hbm.at[high], g_hi),
        (dh_in, dh_sums),
    ]
    copies = [pltpu.make_async_copy(src, dst, sems.at[n]) for n, (src, dst) in enumerate(pairs)]
    for copy in copies:
        copy.start()
    for copy in copies:
        copy.wait()

    def column(masked, i, carry):
        lanes = pl.ds(pl.multiple_of(i * LANES, LANES), LANES)
        dest = i // per_shard
        place = pl.ds(pl.multiple_of((i % per_shard) * LANES, LANES), LANES)
        row_id = lax.broadcasted_iota(jnp.int32, (SUB, LANES), 0)
        f_rows = tap_rows(f_ref, lanes, taps)
        u_rows[pl.ds(0, HALO), :] = f32(left[:, lanes])
        u_rows[pl.ds(HALO, EDGE), :] = f32(u_lo[:, lanes])
        gz_rows[pl.ds(0, EDGE), :] = rounded_product(g_hi[:, lanes], q_hi[:, lanes])
        gz_rows[pl.ds(EDGE, HALO), :] = f32(right[:, lanes])
        gz_lo = rounded_product(g_lo[:, lanes], q_lo[:, lanes])
        g_here = f32(g_lo[:, lanes])
        acc = [None] * taps
        grads_q, grads_u = [], []
        for k in range(n_edge):
            here = slice(k * SUB, (k + 1) * SUB)
            since = row_id + (k * SUB - cut) if masked else None
            parts = back_parts(u_rows, HALO + k * SUB, taps, since)
            for j in range(taps):
                term = gz_lo[here] * parts[j]
                acc[j] = term if k == 0 else acc[j] + term
            grads_q.append(g_here[here] * weighted(parts, f_rows))
            since = row_id + (rows - EDGE + k * SUB - cut) if masked else None
            grads_u.append(weighted(ahead_parts(gz_rows, k * SUB, taps, since), f_rows))
        store_pair(y_ref, 0, 0, lanes, *grads_q)
        store_pair(y_ref, 1, 0, lanes, *grads_u)
        for j in range(taps):
            dh_sums[dest, pl.ds(j, 1), place] = dh_sums[dest, pl.ds(j, 1), place] + jnp.sum(acc[j], axis=0, keepdims=True)
        return carry

    by_boundary(cut, rows, taps, column, q_lo.shape[1] // LANES)
    copies = [pltpu.make_async_copy(y_ref, y_hbm, sems.at[0]), pltpu.make_async_copy(dh_sums, dh_out, sems.at[1])]
    for copy in copies:
        copy.start()
    for copy in copies:
        copy.wait()


ANYWHERE = pl.BlockSpec(memory_space=pl.ANY)
LONG = pl.CostEstimate(flops=1 << 34, bytes_accessed=1 << 20, transcendentals=0)
BRIEF = pl.CostEstimate(flops=1, bytes_accessed=1, transcendentals=0)
ON_CHIP = pl.BlockSpec(memory_space=pltpu.VMEM)
SCALARS = pl.BlockSpec(memory_space=pltpu.SMEM)


def main_part(lengths, f3, query, inner, out_grad, dh, shards, first, count, block):
    rows, width = query.shape
    taps = f3.shape[0]
    base = first // block
    per = width // shards // block
    wide = pl.BlockSpec((rows, block), lambda c: (0, base + c))
    return pl.pallas_call(
        functools.partial(main_kernel, taps),
        out_shape=(
            jax.ShapeDtypeStruct((2, rows - EDGE, count), jnp.bfloat16),
            jax.ShapeDtypeStruct((shards, taps, width // shards), jnp.float32),
            jax.ShapeDtypeStruct((2, 1, rows, width) if dh is None else (1, 1, SUB, LANES), jnp.bfloat16),
        ),
        grid=(count // block,),
        in_specs=[SCALARS, pl.BlockSpec((taps, 1, block), lambda c: (0, 0, base + c)), wide, wide, wide]
        + ([] if dh is None else [ANYWHERE]),
        out_specs=(
            pl.BlockSpec((2, rows - EDGE, block), lambda c: (0, 0, c)),
            pl.BlockSpec((1, taps, block), lambda c: ((base + c) // per, 0, (base + c) % per)),
            ANYWHERE,
        ),
        scratch_shapes=[pltpu.VMEM((rows, LANES), jnp.float32)] * 2,
        input_output_aliases={} if dh is None else {5: 1},
        cost_estimate=BRIEF,
        name=f"grads_{first}",
    )(lengths, f3, query, inner, out_grad, *([] if dh is None else [dh]))


def edge_part(lengths, f3, query, inner, out_grad, left, right, dh):
    rows, width = query.shape
    taps = f3.shape[0]
    edge = pltpu.VMEM((EDGE, width), jnp.bfloat16)
    return pl.pallas_call(
        functools.partial(edge_kernel, taps, rows),
        out_shape=(jax.ShapeDtypeStruct((2, EDGE, width), jnp.bfloat16), jax.ShapeDtypeStruct(dh.shape, dh.dtype)),
        in_specs=[SCALARS, ON_CHIP] + [ANYWHERE] * 3 + [ON_CHIP] * 2 + [ANYWHERE],
        out_specs=(ANYWHERE, ANYWHERE),
        scratch_shapes=[
            edge, edge, edge, edge, edge,
            pltpu.VMEM(dh.shape, dh.dtype),
            pltpu.VMEM((2, EDGE, width), jnp.bfloat16),
            pltpu.VMEM((HALO + EDGE, LANES), jnp.float32),
            pltpu.VMEM((HALO + EDGE, LANES), jnp.float32),
            pltpu.SemaphoreType.DMA((6,)),
        ],
        cost_estimate=BRIEF,
        name="edge_grads",
    )(lengths, f3, query, inner, out_grad, left, right, dh)


def put(out, y, spots):
    for k, (row, lane) in enumerate(spots):
        out = lax.dynamic_update_slice(out, y[k][None, None], (k, 0, row, lane))
    return out


def sent(x, axis, to):
    n = lax.axis_size(axis)
    return lax.ppermute(x, axis, [(i, to(i)) for i in range(n) if 0 <= to(i) < n])


def local(query, inner, out_grad, filters, trace_lengths):
    query, inner, out_grad = query[0], inner[0], out_grad[0]
    rows, width = query.shape
    f3 = jnp.transpose(filters, (1, 0, 2))
    shards = lax.axis_size("ctx")
    eighth = width // sum(part for part, _ in RANGES)

    first, dh, parts = 0, None, []
    for part, block in RANGES:
        count = part * eighth
        y, dh, blank = main_part(trace_lengths, f3, query, inner, out_grad, dh, shards, first, count, block)
        out = blank if first == 0 else out
        parts.append((first, y))
        first += count
    pipe, half = lax.axis_index("pipe"), lax.axis_size("pipe") // 2
    arrived = [(first, sent(y, "pipe", lambda i: i - 1)) for first, y in parts]
    y_two = parts[1][1]
    near = sent(y_two, "pipe", lambda i: 0 if i == half else i - 1 if i > 1 else -1)
    relay = jnp.where(pipe == 0, near, y_two)

    q_head, g_head, u_tail, _ = lax.optimization_barrier((query, out_grad, inner, parts[1][1]))
    left = sent(u_tail[rows - HALO :], "ctx", lambda i: i + 1)
    right = sent((f32(g_head[:HALO]) * f32(q_head[:HALO])).astype(jnp.bfloat16), "ctx", lambda i: i - 1)
    f0, y0 = arrived[0]
    out = put(out, y0, ((EDGE, f0), (0, f0)))
    y_edge, dh = edge_part(trace_lengths, f3, query, inner, out_grad, left, right, dh)
    edge = sent(y_edge, "pipe", lambda i: i - 1)

    dh, relay = lax.optimization_barrier((dh, relay))
    far = sent(relay, "pipe", lambda i: half - 1 if i == 0 else 0 if i == 1 else -1)
    shares = lax.all_to_all(dh, "ctx", split_axis=0, concat_axis=0, tiled=True)
    shares, out = lax.optimization_barrier((shares, out))
    arrived = [arrived[2], (arrived[1][0], jnp.where((pipe == 0) | (pipe == half - 1), far, near))]
    mine = jnp.sum(shares, axis=0)[None]
    last = lax.axis_size("pipe") - 1
    theirs = sent(mine, "pipe", lambda i: last - i)

    for first, y in arrived:
        out = put(out, y, ((EDGE, first), (0, first)))
    out = put(out, edge, ((0, 0), (rows - EDGE, 0)))
    mine, out = lax.optimization_barrier((mine, out))
    return out, mine + theirs


def solution(mesh):
    in_specs = (
        P("pipe", "ctx", None),
        P("pipe", "ctx", None),
        P("pipe", "ctx", None),
        P("pipe", None, None),
        P("pipe", None),
    )
    out_specs = (P(None, "pipe", "ctx", None), P("pipe", None, "ctx"))
    return jax.shard_map(local, mesh=mesh, in_specs=in_specs, out_specs=out_specs, check_vma=False)
```

```python
import functools

import jax
import jax.numpy as jnp
from jax import lax
from jax.experimental import pallas as pl
from jax.experimental.pallas import tpu as pltpu
from jax.sharding import PartitionSpec as P


SUB = 8
LANES = 128
EDGE = 16
HALO = 8
RANGES = ((3, 1024), (3, 1024), (2, 1024))


def f32(x):
    return x.astype(jnp.float32)


def rounded_product(a, b):
    return f32((f32(a) * f32(b)).astype(jnp.bfloat16))


def tap_rows(f_ref, lanes, taps):
    return [jnp.broadcast_to(f_ref[j, :, lanes], (SUB, LANES)) for j in range(taps)]


def back_parts(ref, row, taps, since):
    out = []
    for j in range(taps):
        part = ref[pl.ds(row - j, SUB), :]
        if since is not None and j > 0:
            part = jnp.where((since < 0) | (since >= j), part, 0.0)
        out.append(part)
    return out


def ahead_parts(ref, row, taps, since):
    out = []
    for j in range(taps):
        part = ref[pl.ds(row + j, SUB), :]
        if since is not None and j > 0:
            part = jnp.where((since >= 0) | (since < -j), part, 0.0)
        out.append(part)
    return out


def weighted(parts, f_rows):
    total = f_rows[0] * parts[0]
    for part, row in zip(parts[1:], f_rows[1:], strict=True):
        total = total + row * part
    return total


def store_pair(ref, which, row, lanes, low, high):
    ref[which, pl.ds(row, 2 * SUB), lanes] = jnp.concatenate([low, high], axis=0).astype(jnp.bfloat16)


def boundary(lengths_ref, rows, ctx):
    return lengths_ref[0, 0] - ctx * rows


def by_boundary(cut, rows, taps, body, count, unroll=1):
    near = (cut > -taps) & (cut < rows + taps)

    @pl.when(near)
    def _():
        lax.fori_loop(0, count, functools.partial(body, True), 0, unroll=unroll)

    @pl.when(jnp.logical_not(near))
    def _():
        lax.fori_loop(0, count, functools.partial(body, False), 0, unroll=unroll)


def main_kernel(taps, lengths_ref, f_ref, q_ref, u_ref, g_ref, *rest):
    y_ref, dh_ref, _, u_rows, gz_rows = rest[-5:]
    rows, width = q_ref.shape
    n_tiles, n_edge = rows // SUB, EDGE // SUB
    cut = boundary(lengths_ref, rows, lax.axis_index("ctx"))

    def column(masked, i, carry):
        lanes = pl.ds(pl.multiple_of(i * LANES, LANES), LANES)
        row_id = lax.broadcasted_iota(jnp.int32, (SUB, LANES), 0)
        f_rows = tap_rows(f_ref, lanes, taps)
        for k in range(0, n_tiles, 2):
            two = pl.ds(k * SUB, 2 * SUB)
            u_rows[two, :] = f32(u_ref[two, lanes])
            gz_rows[two, :] = rounded_product(g_ref[two, lanes], q_ref[two, lanes])
        acc = [jnp.zeros((SUB, LANES), jnp.float32) for _ in range(taps)]
        for k in range(0, n_tiles, 2):
            g_two = f32(g_ref[pl.ds(k * SUB, 2 * SUB), lanes])
            grads_q, grads_u = [], []
            for half in range(2):
                row = (k + half) * SUB
                since = row_id + (row - cut) if masked else None
                if k >= n_edge:
                    parts = back_parts(u_rows, row, taps, since)
                    gz_here = gz_rows[pl.ds(row, SUB), :]
                    for j in range(taps):
                        acc[j] = acc[j] + gz_here * parts[j]
                    grads_q.append(g_two[half * SUB : (half + 1) * SUB] * weighted(parts, f_rows))
                if k < n_tiles - n_edge:
                    grads_u.append(weighted(ahead_parts(gz_rows, row, taps, since), f_rows))
            if grads_q:
                store_pair(y_ref, 0, (k - n_edge) * SUB, lanes, *grads_q)
            if grads_u:
                store_pair(y_ref, 1, k * SUB, lanes, *grads_u)
        for j in range(taps):
            dh_ref[0, pl.ds(j, 1), lanes] = jnp.sum(acc[j], axis=0, keepdims=True)
        return carry

    by_boundary(cut, rows, taps, column, width // LANES)


def edge_kernel(taps, rows, lengths_ref, f_ref, q_hbm, u_hbm, g_hbm, left, right, dh_in, y_hbm, dh_out, *scratch):
    q_lo, u_lo, g_lo, q_hi, g_hi, dh_sums, y_ref, u_rows, gz_rows, sems = scratch
    n_edge = EDGE // SUB
    per_shard = dh_in.shape[2] // LANES
    cut = boundary(lengths_ref, rows, lax.axis_index("ctx"))
    low, high = pl.ds(0, EDGE), pl.ds(rows - EDGE, EDGE)
    pairs = [
        (q_hbm.at[low], q_lo), (u_hbm.at[low], u_lo), (g_hbm.at[low], g_lo), (q_hbm.at[high], q_hi), (g_hbm.at[high], g_hi),
        (dh_in, dh_sums),
    ]
    copies = [pltpu.make_async_copy(src, dst, sems.at[n]) for n, (src, dst) in enumerate(pairs)]
    for copy in copies:
        copy.start()
    for copy in copies:
        copy.wait()

    def column(masked, i, carry):
        lanes = pl.ds(pl.multiple_of(i * LANES, LANES), LANES)
        dest = i // per_shard
        place = pl.ds(pl.multiple_of((i % per_shard) * LANES, LANES), LANES)
        row_id = lax.broadcasted_iota(jnp.int32, (SUB, LANES), 0)
        f_rows = tap_rows(f_ref, lanes, taps)
        u_rows[pl.ds(0, HALO), :] = f32(left[:, lanes])
        u_rows[pl.ds(HALO, EDGE), :] = f32(u_lo[:, lanes])
        gz_rows[pl.ds(0, EDGE), :] = rounded_product(g_hi[:, lanes], q_hi[:, lanes])
        gz_rows[pl.ds(EDGE, HALO), :] = f32(right[:, lanes])
        gz_lo = rounded_product(g_lo[:, lanes], q_lo[:, lanes])
        g_here = f32(g_lo[:, lanes])
        acc = [None] * taps
        grads_q, grads_u = [], []
        for k in range(n_edge):
            here = slice(k * SUB, (k + 1) * SUB)
            since = row_id + (k * SUB - cut) if masked else None
            parts = back_parts(u_rows, HALO + k * SUB, taps, since)
            for j in range(taps):
                term = gz_lo[here] * parts[j]
                acc[j] = term if k == 0 else acc[j] + term
            grads_q.append(g_here[here] * weighted(parts, f_rows))
            since = row_id + (rows - EDGE + k * SUB - cut) if masked else None
            grads_u.append(weighted(ahead_parts(gz_rows, k * SUB, taps, since), f_rows))
        store_pair(y_ref, 0, 0, lanes, *grads_q)
        store_pair(y_ref, 1, 0, lanes, *grads_u)
        for j in range(taps):
            dh_sums[dest, pl.ds(j, 1), place] = dh_sums[dest, pl.ds(j, 1), place] + jnp.sum(acc[j], axis=0, keepdims=True)
        return carry

    by_boundary(cut, rows, taps, column, q_lo.shape[1] // LANES, unroll=4)
    copies = [pltpu.make_async_copy(y_ref, y_hbm, sems.at[0]), pltpu.make_async_copy(dh_sums, dh_out, sems.at[1])]
    for copy in copies:
        copy.start()
    for copy in copies:
        copy.wait()


ANYWHERE = pl.BlockSpec(memory_space=pl.ANY)
LONG = pl.CostEstimate(flops=1 << 34, bytes_accessed=1 << 20, transcendentals=0)
BRIEF = pl.CostEstimate(flops=1, bytes_accessed=1, transcendentals=0)
ON_CHIP = pl.BlockSpec(memory_space=pltpu.VMEM)
SCALARS = pl.BlockSpec(memory_space=pltpu.SMEM)


def main_part(lengths, f3, query, inner, out_grad, dh, shards, first, count, block):
    rows, width = query.shape
    taps = f3.shape[0]
    base = first // block
    per = width // shards // block
    wide = pl.BlockSpec((rows, block), lambda c: (0, base + c))
    return pl.pallas_call(
        functools.partial(main_kernel, taps),
        out_shape=(
            jax.ShapeDtypeStruct((2, rows - EDGE, count), jnp.bfloat16),
            jax.ShapeDtypeStruct((shards, taps, width // shards), jnp.float32),
            jax.ShapeDtypeStruct((2, 1, rows, width) if dh is None else (1, 1, SUB, LANES), jnp.bfloat16),
        ),
        grid=(count // block,),
        in_specs=[SCALARS, pl.BlockSpec((taps, 1, block), lambda c: (0, 0, base + c)), wide, wide, wide]
        + ([] if dh is None else [ANYWHERE]),
        out_specs=(
            pl.BlockSpec((2, rows - EDGE, block), lambda c: (0, 0, c)),
            pl.BlockSpec((1, taps, block), lambda c: ((base + c) // per, 0, (base + c) % per)),
            ANYWHERE,
        ),
        scratch_shapes=[pltpu.VMEM((rows, LANES), jnp.float32)] * 2,
        input_output_aliases={} if dh is None else {5: 1},
        cost_estimate=BRIEF,
        name=f"grads_{first}",
    )(lengths, f3, query, inner, out_grad, *([] if dh is None else [dh]))


def edge_part(lengths, f3, query, inner, out_grad, left, right, dh):
    rows, width = query.shape
    taps = f3.shape[0]
    edge = pltpu.VMEM((EDGE, width), jnp.bfloat16)
    return pl.pallas_call(
        functools.partial(edge_kernel, taps, rows),
        out_shape=(jax.ShapeDtypeStruct((2, EDGE, width), jnp.bfloat16), jax.ShapeDtypeStruct(dh.shape, dh.dtype)),
        in_specs=[SCALARS, ON_CHIP] + [ANYWHERE] * 3 + [ON_CHIP] * 2 + [ANYWHERE],
        out_specs=(ANYWHERE, ANYWHERE),
        scratch_shapes=[
            edge, edge, edge, edge, edge,
            pltpu.VMEM(dh.shape, dh.dtype),
            pltpu.VMEM((2, EDGE, width), jnp.bfloat16),
            pltpu.VMEM((HALO + EDGE, LANES), jnp.float32),
            pltpu.VMEM((HALO + EDGE, LANES), jnp.float32),
            pltpu.SemaphoreType.DMA((6,)),
        ],
        cost_estimate=BRIEF,
        name="edge_grads",
    )(lengths, f3, query, inner, out_grad, left, right, dh)


def put(out, y, spots):
    for k, (row, lane) in enumerate(spots):
        out = lax.dynamic_update_slice(out, y[k][None, None], (k, 0, row, lane))
    return out


def sent(x, axis, to):
    n = lax.axis_size(axis)
    return lax.ppermute(x, axis, [(i, to(i)) for i in range(n) if 0 <= to(i) < n])


def local(query, inner, out_grad, filters, trace_lengths):
    query, inner, out_grad = query[0], inner[0], out_grad[0]
    rows, width = query.shape
    f3 = jnp.transpose(filters, (1, 0, 2))
    shards = lax.axis_size("ctx")
    eighth = width // sum(part for part, _ in RANGES)

    pipe, half = lax.axis_index("pipe"), lax.axis_size("pipe") // 2
    back = lambda i: i - 1
    dh, parts, first = None, [], 0
    for n, (part, block) in enumerate(RANGES):
        if n == 2:
            dh, out, _, _ = lax.optimization_barrier((dh, out, u_tail, gz_head))
        y, dh, blank = main_part(trace_lengths, f3, query, inner, out_grad, dh, shards, first, part * eighth, block)
        if n == 0:
            out = blank
        parts.append((first, y))
        first += part * eighth
        if n == 1:
            (f0, y0), (f1, y_two) = parts
            a0 = sent(y0, "pipe", back)
            near = sent(y_two, "pipe", lambda i: 0 if i == half else i - 1 if i > 1 else -1)
            relay = jnp.where(pipe == 0, near, y_two)
            q_head, g_head, u_tail, _ = lax.optimization_barrier((query, out_grad, inner, y_two))
            u_tail = u_tail[rows - HALO :]
            gz_head = (f32(g_head[:HALO]) * f32(q_head[:HALO])).astype(jnp.bfloat16)
            left, right = sent(u_tail, "ctx", lambda i: i + 1), sent(gz_head, "ctx", back)
            out = put(out, a0, ((EDGE, f0), (0, f0)))
    f2, a2 = parts[2][0], sent(parts[2][1], "pipe", back)
    y_edge, dh = edge_part(trace_lengths, f3, query, inner, out_grad, left, right, dh)
    edge = sent(y_edge, "pipe", back)
    dh, relay = lax.optimization_barrier((dh, relay))
    far = sent(relay, "pipe", lambda i: half - 1 if i == 0 else 0 if i == 1 else -1)
    shares = lax.all_to_all(dh, "ctx", split_axis=0, concat_axis=0, tiled=True)
    out = put(out, a2, ((EDGE, f2), (0, f2)))
    shares, out = lax.optimization_barrier((shares, out))
    mine = jnp.sum(shares, axis=0)[None]
    last = lax.axis_size("pipe") - 1
    theirs = sent(mine, "pipe", lambda i: last - i)
    out = put(out, jnp.where((pipe == 0) | (pipe == half - 1), far, near), ((EDGE, f1), (0, f1)))
    out = put(out, edge, ((0, 0), (rows - EDGE, 0)))
    mine, out = lax.optimization_barrier((mine, out))
    return out, mine + theirs


def solution(mesh):
    in_specs = (
        P("pipe", "ctx", None),
        P("pipe", "ctx", None),
        P("pipe", "ctx", None),
        P("pipe", None, None),
        P("pipe", None),
    )
    out_specs = (P(None, "pipe", "ctx", None), P("pipe", None, "ctx"))
    return jax.shard_map(local, mesh=mesh, in_specs=in_specs, out_specs=out_specs, check_vma=False)
```
